256 devices in a mesh: half: 2 (over core), dev: 128 (over y, x, z).
Axes of the slice: x: 4, y: 4, z: 8, core: 2. Of those that a mesh axis runs over, the one named last changes fastest.
Arguments:
- field_mix: float32 [32, 32], P('half'), may hold values from -1 to 1
- alm: bfloat16 [1024, 2, 32, 2048], P('dev', None, 'half'), may hold values from -6 to 6
- legendre: bfloat16 [1024, 2048, 128], P('dev'), may hold values from -0.125 to 0.125
- order_ids: int32 [1024], replicated, may hold values from 0 to 1023, each once
- fetch_list: int32 [128, 128, 2], replicated, may hold values from -1 to 31, as said below
- scan_tiles: int32 [512, 32], P('dev'), may hold values from 0 to 255, as said below
- block_tile: int32 [512, 32], P('dev'), may hold values from 0 to 31
- block_pix: int32 [512, 16384], P('dev'), may hold values from -1 to 127, as said below
- noise_kernel: float32 [512, 512], P('dev'), may hold values from -0.24 to 0.24
- scan_weight: float32 [512], P('dev'), may hold values from 0.1 to 1
Outputs:
- binned: float32 [128, 32, 4096], P('dev', 'half')
The draws below stay inside these ranges and needn't reach their ends.
Inputs may be any that keep to these rules, and one draw needn't show every extreme that they name: `fetch_list`: entry [d, e, k] is the index, among the 32 tiles of device d, of the tile that device e fetches from d in slot k, or -1 for an empty slot; the live slots of one pair come first and name distinct tiles; every device fills all 2 slots from at least one source. `scan_tiles`: entry [n, i] is a slot source 2 + k whose fetch_list[source, n div 4, k] is not -1. `block_pix`: -1 marks a flagged sample.
All inputs are finite; a program needn't handle non-finite values.
Results may differ from the reference program's by a relative error of at most 0.007.
Values may be sent and summed in bfloat16 or wider, within the bound.
No kernel may reach another device: no remote copies, remote signals or barrier semaphores. Data moves between devices by JAX's collectives and lax.ppermute only.
A program may use at most 128 MiB of HBM per device.

```python
import math
import jax
import jax.numpy as jnp
from jax import lax

FIELDS = 32
ELLS = 2048
NPHI = 4096
TILE = 128
BLK = 512
KW = 512
CAP = 2
TPS = 32
NBLK = 32
SCAN_DEV = 4
ORDERS = 1024
CYCLES = 128
SCANS = 512
TILES_DEV = 32
N_DEV = 128


def owner_plan(key):
    plan_key = jax.random.fold_in(key, 7001)
    count_key, hot_key, tile_key, order_key = jax.random.split(plan_key, 4)
    count_draw = jax.random.randint(count_key, (N_DEV, N_DEV), 0, 4)
    counts = jnp.where(count_draw == 3, CAP, jnp.minimum(count_draw, 1))
    hottest = jax.random.randint(hot_key, (N_DEV,), 0, N_DEV)
    counts = jnp.where(jnp.arange(N_DEV)[None, :] == hottest[:, None], CAP, counts)
    scores = jax.random.randint(tile_key, (N_DEV, N_DEV, TILES_DEV), 0, 1 << 20) * TILES_DEV + jnp.arange(TILES_DEV)[None, None, :]
    ranked = jnp.argsort(scores, axis=-1)[:, :, :CAP]
    live_slot = jnp.arange(CAP)[None, None, :] < counts[:, :, None]
    by_dest = jnp.where(live_slot, ranked, -1)
    fetch_table = jnp.transpose(by_dest, (1, 0, 2)).astype(jnp.int32)
    live_flat = live_slot.reshape(N_DEV, N_DEV * CAP)
    slot_total = N_DEV * CAP
    slot_iota = jnp.arange(slot_total)
    shuffle = jax.random.randint(order_key, (N_DEV, slot_total), 0, 1 << 16) * slot_total + slot_iota[None, :]
    sort_key = jnp.where(live_flat, shuffle, (1 << 16) * slot_total + slot_iota[None, :])
    used_list = jnp.argsort(sort_key, axis=-1)
    used_count = jnp.sum(live_flat.astype(jnp.int32), axis=-1)
    entry_iota = jnp.arange(SCAN_DEV * TPS)
    picked = entry_iota[None, :] % used_count[:, None]
    scan_list = jnp.take_along_axis(used_list, picked, axis=1).reshape(N_DEV * SCAN_DEV, TPS)
    return (fetch_table, scan_list.astype(jnp.int32))


def draw_fetch_list(key, part):
    return owner_plan(key)[0]


def draw_scan_tiles(key, part):
    return owner_plan(key)[1]


def draw_block_tile(key, part):
    order_key = jax.random.fold_in(key, 7003)
    scores = jax.random.randint(order_key, (SCANS, NBLK), 0, 1 << 16) * NBLK + jnp.arange(NBLK)[None, :]
    shuffled = jnp.argsort(scores, axis=-1)
    return (shuffled % TPS).astype(jnp.int32)


def draw_block_pix(key, part):
    flag_key, pixel_key = jax.random.split(jax.random.fold_in(key, 7002))
    pixels = jax.random.randint(pixel_key, (SCANS, NBLK * BLK), 0, TILE)
    flagged = jax.random.randint(flag_key, (SCANS, NBLK * BLK), 0, 8) == 0
    return jnp.where(flagged, -1, pixels).astype(jnp.int32)


def steps_of(own_key, extent, cuts, smallest, top_value):
    gain = 1.0
    for axis_at, shards_of in cuts:
        steps = jax.random.uniform(jax.random.fold_in(jax.random.fold_in(own_key, 6), axis_at), (shards_of,), jnp.float32, smallest / len(cuts), top_value / len(cuts))
        gain = gain * jnp.repeat(jnp.exp(steps), extent[axis_at] // shards_of).reshape((-1,) + (1,) * (len(extent) - 1 - axis_at))
    return gain


def gaussian(rng, extent, width, reach, cuts=(), held_as=jnp.bfloat16):
    values = width * jax.random.normal(rng, extent, jnp.float32)
    if cuts:
        values = values * steps_of(rng, extent, cuts, -0.22, 0.18)
    return jnp.clip(values, -reach, reach).astype(held_as)


def setup_inputs(seed: int = 0) -> dict:
    keys = jax.random.split(jax.random.key(seed), 11)
    return {
        "field_mix": gaussian(keys[0], (FIELDS, FIELDS), FIELDS ** -0.5, 1.0, ((0, 2),), jnp.float32),
        "alm": gaussian(keys[1], (ORDERS, 2, FIELDS, ELLS), 1.0, 6.0, ((0, 128), (2, 2))),
        "legendre": gaussian(keys[2], (ORDERS, ELLS, CYCLES), ELLS ** -0.5, 0.125, ((0, 128),)),
        "order_ids": jax.random.permutation(keys[3], ORDERS).astype(jnp.int32),
        "fetch_list": draw_fetch_list(jax.random.fold_in(keys[10], 71), 0),
        "scan_tiles": draw_scan_tiles(jax.random.fold_in(keys[10], 71), 0),
        "block_tile": draw_block_tile(jax.random.fold_in(keys[10], 71), 0),
        "block_pix": draw_block_pix(jax.random.fold_in(keys[10], 71), 0),
        "noise_kernel": gaussian(keys[8], (SCANS, KW), 0.04, 0.24, ((0, 128),), jnp.float32),
        "scan_weight": jnp.clip(jnp.exp(math.log(1.0) - 2.3025851 * jax.random.uniform(keys[9], (SCANS,), jnp.float32) ** steps_of(keys[9], (SCANS,), ((0, 128),), -0.2, 0.2)), 0.1, 1.0),
    }


def reference(field_mix, alm, legendre, order_ids, fetch_list, scan_tiles, block_tile, block_pix, noise_kernel, scan_weight):
    highest = lax.Precision.HIGHEST

    def order_cycles(operands):
        coeffs, table = operands
        mixed_alm = jnp.einsum('fg,cgl->cfl', field_mix, coeffs.astype(jnp.float32), precision=highest).astype(jnp.bfloat16)
        return jnp.einsum('cfl,lr->rcf', mixed_alm.astype(jnp.float32), table.astype(jnp.float32)).astype(jnp.bfloat16)
    cycle_coeff = lax.map(order_cycles, (alm, legendre))
    by_cycle = jnp.transpose(cycle_coeff, (1, 0, 2, 3))
    pixel_iota = jnp.arange(NPHI, dtype=jnp.int32)
    phase_steps = order_ids[:, None] * (2 * pixel_iota[None, :] + 1) % (2 * NPHI)
    angles = phase_steps.astype(jnp.float32) * (math.pi / NPHI)
    weights = jnp.where(order_ids == 0, 1.0, 2.0).astype(jnp.float32) / math.sqrt(2.0 * ORDERS)
    fourier = jnp.stack([weights[:, None] * jnp.cos(angles), -weights[:, None] * jnp.sin(angles)], axis=1).astype(jnp.bfloat16)
    fourier_wide = fourier.astype(jnp.float32)

    def cycle_pixels(coeffs):
        return jnp.einsum('scf,scj->fj', coeffs.astype(jnp.float32), fourier_wide).astype(jnp.bfloat16)
    cycle_maps = lax.map(cycle_pixels, by_cycle)
    flat_map = jnp.transpose(cycle_maps, (1, 0, 2)).reshape(FIELDS, CYCLES * NPHI)
    scan_iota = jnp.arange(SCANS, dtype=jnp.int32)
    holder = scan_iota // SCAN_DEV
    slot_index = jnp.take_along_axis(scan_tiles, block_tile, axis=1)
    source = slot_index // CAP
    within = slot_index % CAP
    local_tile = fetch_list[source, holder[:, None], within]
    global_tile = source * TILES_DEV + local_tile
    pixels = block_pix.reshape(SCANS, NBLK, BLK)
    valid_mask = (pixels >= 0).reshape(SCANS, NBLK * BLK)
    target = (global_tile[:, :, None] * TILE + jnp.maximum(pixels, 0)).reshape(SCANS, NBLK * BLK)
    scan_length = NBLK * BLK
    padded_length = 1 << int(math.ceil(math.log2(scan_length + KW)))
    taps = lax.optimization_barrier(noise_kernel.astype(jnp.bfloat16)).astype(jnp.float32)
    response = jnp.zeros((SCANS, padded_length), jnp.float32)
    response = response.at[:, :KW].set(taps)
    response = response.at[:, padded_length - KW + 1:].set(taps[:, 1:][:, ::-1])

    def scan_step(total, operands):
        spots, mask_row, answer, weight = operands
        samples = jnp.where(mask_row[None, :], flat_map[:, spots], 0).astype(jnp.float32)
        spectrum = jnp.fft.rfft(samples, n=padded_length, axis=-1) * jnp.fft.rfft(answer)[None, :]
        filtered = jnp.fft.irfft(spectrum, n=padded_length, axis=-1)[:, :scan_length]
        weighted = lax.optimization_barrier((weight * filtered).astype(jnp.bfloat16)).astype(jnp.float32)
        destination = jnp.where(mask_row, spots, CYCLES * NPHI)
        total = total.at[:, destination].add(weighted, mode='drop')
        return (total, None)
    initial = jnp.zeros((FIELDS, CYCLES * NPHI), jnp.float32)
    binned_flat, unused = lax.scan(scan_step, initial, (target, valid_mask, response, scan_weight))
    return binned_flat.reshape(FIELDS, CYCLES, NPHI).transpose(1, 0, 2)
```

```python
import math

import jax
import jax.numpy as jnp
from jax import lax
from jax.experimental import pallas as pl
from jax.experimental.pallas import tpu as pltpu
from jax.sharding import PartitionSpec as P

NPHI = 4096
TILE = 128
BLK = 512
HALF_BLK = 256
F32 = jnp.float32
BF16 = jnp.bfloat16
VMEM_LIMIT = 60 * 1024 * 1024


def legendre_kernel(alm_hbm, leg_hbm, out_ref, alm_buf, leg_buf, sems):
    orders = leg_buf.shape[0]
    copies = []
    for s in range(orders):
        a = pltpu.make_async_copy(alm_hbm.at[s], alm_buf.at[s], sems.at[0, s])
        b = pltpu.make_async_copy(leg_hbm.at[s], leg_buf.at[s], sems.at[1, s])
        a.start()
        b.start()
        copies.append((a, b))
    for s in range(orders):
        copies[s][0].wait()
        copies[s][1].wait()
        rows = alm_buf.shape[1]
        out_ref[pl.ds(s * rows, rows), :] = jnp.dot(
            alm_buf[s], leg_buf[s], preferred_element_type=F32
        )


def contract_ells(alm, legendre):
    orders, parts, fields, ells = alm.shape
    cycles = legendre.shape[2]
    rows = parts * fields
    return pl.pallas_call(
        legendre_kernel,
        out_shape=jax.ShapeDtypeStruct((orders * rows, cycles), F32),
        in_specs=[pl.BlockSpec(memory_space=pl.ANY), pl.BlockSpec(memory_space=pl.ANY)],
        scratch_shapes=[
            pltpu.VMEM((orders, rows, ells), BF16),
            pltpu.VMEM((orders, ells, cycles), BF16),
            pltpu.SemaphoreType.DMA((2, orders)),
        ],
        compiler_params=pltpu.CompilerParams(vmem_limit_bytes=VMEM_LIMIT),
        name="contract_ells",
    )(alm.reshape(orders, rows, ells), legendre)


def mix_kernel(own_ref, other_ref, mix_ref, out_ref):
    fields = mix_ref.shape[1]
    rows = own_ref.shape[0]
    highest = lax.Precision.HIGHEST
    row_group = lax.broadcasted_iota(jnp.int32, (rows, rows), 0) // fields
    col_group = lax.broadcasted_iota(jnp.int32, (rows, rows), 1) // fields
    spread = (
        lax.broadcasted_iota(jnp.int32, (rows, fields), 0) % fields
        == lax.broadcasted_iota(jnp.int32, (rows, fields), 1)
    ).astype(F32)
    spread_t = (
        lax.broadcasted_iota(jnp.int32, (fields, rows), 1) % fields
        == lax.broadcasted_iota(jnp.int32, (fields, rows), 0)
    ).astype(F32)

    def mixed(mix, values):
        wide = jnp.dot(
            jnp.dot(spread, mix, precision=highest, preferred_element_type=F32),
            spread_t,
            precision=highest,
            preferred_element_type=F32,
        )
        wide = jnp.where(row_group == col_group, wide, 0.0)
        return jnp.dot(wide, values, precision=highest, preferred_element_type=F32)

    total = mixed(mix_ref[0], own_ref[...]) + mixed(mix_ref[1], other_ref[...])
    by_cycle = total.T.astype(BF16)
    lanes = out_ref.shape[2]
    for p in range(out_ref.shape[1]):
        out_ref[:, p, :] = by_cycle[:, p * lanes : (p + 1) * lanes]


def mix_fields(own, other, mix_pair):
    rows, cycles = own.shape
    return pl.pallas_call(
        mix_kernel,
        out_shape=jax.ShapeDtypeStruct((cycles, rows // 128, 128), BF16),
        compiler_params=pltpu.CompilerParams(vmem_limit_bytes=VMEM_LIMIT),
        name="mix_fields",
    )(own, other, mix_pair)


def synth_kernel(owner_ref, coeff_ref, turn_ref, table_ref, out_ref, lhs_ref, map_ref):
    devices, groups, lanes = coeff_ref.shape
    tiles, fields = map_ref.shape[0], map_ref.shape[1]
    slots = turn_ref.shape[2]
    per_group = slots // groups
    k_half = slots * devices
    flipped = [coeff_ref[:, g, :].astype(F32).T for g in range(groups)]
    for s in range(slots):
        block = flipped[s // per_group]
        at = (s % per_group) * 2 * fields
        real = block[at : at + fields]
        imag = block[at + fields : at + 2 * fields]
        for j in range(tiles):
            cos_row = turn_ref[0, j, s : s + 1, :]
            sin_row = turn_ref[1, j, s : s + 1, :]
            rows = pl.ds(j * fields, fields)
            lhs_ref[rows, pl.ds(s * devices, devices)] = (real * cos_row - imag * sin_row).astype(
                BF16
            )
            lhs_ref[rows, pl.ds(k_half + s * devices, devices)] = (
                real * sin_row + imag * cos_row
            ).astype(BF16)
    pixels = jnp.dot(lhs_ref[...], table_ref[...], preferred_element_type=F32).astype(BF16)
    map_ref[...] = pixels.reshape(tiles, fields, TILE)
    capacity = out_ref.shape[1]

    def pick(e, carry):
        for k in range(capacity):
            g = jnp.maximum(owner_ref[k, e], 0)
            out_ref[e, k] = map_ref[g]
        return carry

    lax.fori_loop(0, out_ref.shape[0], pick, 0, unroll=8)


def synthesize(owner_row, coeff, turns, table, fields):
    capacity, devices = owner_row.shape
    tiles = turns.shape[1]
    k_total = table.shape[0]
    return pl.pallas_call(
        synth_kernel,
        out_shape=jax.ShapeDtypeStruct((devices, capacity, fields, TILE), BF16),
        in_specs=[
            pl.BlockSpec(memory_space=pltpu.SMEM),
            pl.BlockSpec(memory_space=pltpu.VMEM),
            pl.BlockSpec(memory_space=pltpu.VMEM),
            pl.BlockSpec(memory_space=pltpu.VMEM),
        ],
        scratch_shapes=[
            pltpu.VMEM((tiles * fields, k_total), BF16),
            pltpu.VMEM((tiles, fields, TILE), BF16),
        ],
        compiler_params=pltpu.CompilerParams(vmem_limit_bytes=VMEM_LIMIT),
        name="synthesize",
    )(owner_row, coeff, turns, table)


def band_kernel(row_ref, out_ref):
    rows, width = out_ref.shape[1], out_ref.shape[2]
    wide = jnp.broadcast_to(row_ref[0], (rows, width))
    out_ref[0] = pltpu.roll(wide, 0, 1, stride=1, stride_axis=0).astype(BF16)


def band_strips(rows):
    scans, _, width = rows.shape
    return pl.pallas_call(
        band_kernel,
        grid=(scans,),
        out_shape=jax.ShapeDtypeStruct((scans, HALF_BLK, width), BF16),
        in_specs=[pl.BlockSpec((1, 1, width), lambda n: (n, 0, 0))],
        out_specs=pl.BlockSpec((1, HALF_BLK, width), lambda n: (n, 0, 0)),
        compiler_params=pltpu.CompilerParams(vmem_limit_bytes=VMEM_LIMIT),
        name="band_strips",
    )(rows)


def scan_kernel(
    list_ref, entry_ref, weight_ref, tiles_ref, pix_ref, strip_ref, out_ref, pad_ref, wtd_ref, sum_ref
):
    n = pl.program_id(0)
    fields = tiles_ref.shape[1]
    blocks = entry_ref.shape[1]
    halves = 2 * blocks
    edge = 2 * fields

    @pl.when(n == 0)
    def _():
        sum_ref[...] = jnp.zeros_like(sum_ref)
        pad_ref[pl.ds(0, edge), :] = jnp.zeros((edge, HALF_BLK), BF16)
        pad_ref[pl.ds(edge + halves * fields, edge), :] = jnp.zeros((edge, HALF_BLK), BF16)

    per_half = HALF_BLK // TILE
    quarters = BLK // TILE

    def gather(b, carry):
        slot = list_ref[n, entry_ref[n, b]]
        tile = tiles_ref[slot].astype(F32)
        for q in range(quarters):
            row = pix_ref[0, pl.ds(b * quarters + q, 1), :]
            at = jnp.broadcast_to(row, (8, TILE))
            live = at >= 0
            index = jnp.maximum(at, 0)
            parts = [
                jnp.where(
                    live,
                    jnp.take_along_axis(
                        tile[8 * i : 8 * i + 8], index, axis=1, mode="promise_in_bounds"
                    ),
                    0.0,
                )
                for i in range(fields // 8)
            ]
            start = pl.multiple_of(edge + (2 * b + q // per_half) * fields, fields)
            pad_ref[pl.ds(start, fields), pl.ds((q % per_half) * TILE, TILE)] = jnp.concatenate(
                parts, axis=0
            ).astype(BF16)
        return carry

    lax.fori_loop(0, blocks, gather, 0, unroll=4)
    total = None
    for d in range(-2, 3):
        term = jnp.dot(
            pad_ref[pl.ds(edge - d * fields, halves * fields), :],
            strip_ref[0, :, pl.ds((d + 2) * HALF_BLK, HALF_BLK)],
            preferred_element_type=F32,
        )
        total = term if total is None else total + term
    wtd_ref[...] = (weight_ref[n] * total).astype(BF16)
    pixel_iota = lax.broadcasted_iota(jnp.int32, (TILE, TILE), 0)

    def bin_block(b, carry):
        slot = list_ref[n, entry_ref[n, b]]
        partial = None
        for q in range(quarters):
            row = pix_ref[0, pl.ds(b * quarters + q, 1), :]
            hot = (pixel_iota == row).astype(F32).astype(BF16)
            start = pl.multiple_of((2 * b + q // per_half) * fields, fields)
            values = wtd_ref[pl.ds(start, fields), pl.ds((q % per_half) * TILE, TILE)]
            term = lax.dot_general(
                values, hot, (((1,), (1,)), ((), ())), preferred_element_type=F32
            )
            partial = term if partial is None else partial + term
        sum_ref[slot] = sum_ref[slot] + partial
        return carry

    lax.fori_loop(0, blocks, bin_block, 0, unroll=4)

    @pl.when(n == pl.num_programs(0) - 1)
    def _():
        out_ref[...] = sum_ref[...].astype(BF16)


def scan_stage(scan_tiles, block_tile, scan_weight, tiles, pix, strips):
    slots, fields, _ = tiles.shape
    scans, blocks = block_tile.shape
    rows = blocks * BLK // TILE
    width = strips.shape[2]
    smem = pl.BlockSpec(memory_space=pltpu.SMEM)
    whole = pl.BlockSpec((slots, fields, TILE), lambda n: (0, 0, 0))
    return pl.pallas_call(
        scan_kernel,
        grid=(scans,),
        out_shape=jax.ShapeDtypeStruct((slots, fields, TILE), BF16),
        in_specs=[
            smem,
            smem,
            smem,
            whole,
            pl.BlockSpec((1, rows, TILE), lambda n: (n, 0, 0)),
            pl.BlockSpec((1, HALF_BLK, width), lambda n: (n, 0, 0)),
        ],
        out_specs=whole,
        scratch_shapes=[
            pltpu.VMEM(((2 * blocks + 4) * fields, HALF_BLK), BF16),
            pltpu.VMEM((2 * blocks * fields, HALF_BLK), BF16),
            pltpu.VMEM((slots, fields, TILE), F32),
        ],
        compiler_params=pltpu.CompilerParams(
            vmem_limit_bytes=VMEM_LIMIT, dimension_semantics=("arbitrary",)
        ),
        name="scan_stage",
    )(scan_tiles, block_tile, scan_weight, tiles, pix, strips)


def owner_kernel(owner_ref, back_ref, out_ref, sum_ref):
    capacity, devices = owner_ref.shape
    tiles = sum_ref.shape[1] - 1
    sum_ref[...] = jnp.zeros_like(sum_ref)

    def add(e, carry):
        for k in range(capacity):
            g = owner_ref[k, e]
            g = jnp.where(g < 0, tiles, g)
            sum_ref[k, g] = sum_ref[k, g] + back_ref[e, k].astype(F32)
        return carry

    lax.fori_loop(0, devices, add, 0, unroll=8)
    for g in range(tiles):
        total = sum_ref[0, g]
        for k in range(1, capacity):
            total = total + sum_ref[k, g]
        out_ref[0, :, pl.ds(g * TILE, TILE)] = total


def owner_sum(owner_row, returned):
    devices, capacity, fields, _ = returned.shape
    tiles = NPHI // TILE
    return pl.pallas_call(
        owner_kernel,
        out_shape=jax.ShapeDtypeStruct((1, fields, NPHI), F32),
        in_specs=[pl.BlockSpec(memory_space=pltpu.SMEM), pl.BlockSpec(memory_space=pltpu.VMEM)],
        scratch_shapes=[pltpu.VMEM((capacity, tiles + 1, fields, TILE), F32)],
        compiler_params=pltpu.CompilerParams(vmem_limit_bytes=VMEM_LIMIT),
        name="owner_sum",
    )(owner_row, returned)


def local(
    field_mix,
    alm,
    legendre,
    order_ids,
    fetch_list,
    scan_tiles,
    block_tile,
    block_pix,
    noise_kernel,
    scan_weight,
):
    half = lax.axis_index("half")
    position = lax.axis_index("dev")
    devices = fetch_list.shape[0]
    fields = alm.shape[2]
    slots = alm.shape[0]
    order_count = order_ids.shape[0]
    scans = block_pix.shape[0]
    tile_count = NPHI // TILE

    own = contract_ells(alm, legendre)
    other = lax.ppermute(own, "half", [(0, 1), (1, 0)])
    low, high = field_mix[:, :fields], field_mix[:, fields:]
    mix_pair = jnp.stack(
        [jnp.where(half == 0, low, high), jnp.where(half == 0, high, low)], axis=0
    )
    sent = mix_fields(own, other, mix_pair)
    coeff = lax.all_to_all(sent, "dev", split_axis=0, concat_axis=0, tiled=True)

    ids = order_ids.reshape(devices, slots).T
    tile_iota = jnp.arange(tile_count, dtype=jnp.int32)
    turn_angle = ((ids[None] * tile_iota[:, None, None]) % tile_count).astype(F32) * (
        2.0 * math.pi / tile_count
    )
    turns = jnp.stack([jnp.cos(turn_angle), jnp.sin(turn_angle)], axis=0)
    flat_ids = ids.reshape(-1)
    pixel_iota = jnp.arange(TILE, dtype=jnp.int32)
    steps = flat_ids[:, None] * (2 * pixel_iota[None, :] + 1) % (2 * NPHI)
    angles = steps.astype(F32) * (math.pi / NPHI)
    weights = jnp.where(flat_ids == 0, 1.0, 2.0).astype(F32) / math.sqrt(2.0 * order_count)
    table = jnp.concatenate(
        [weights[:, None] * jnp.cos(angles), -weights[:, None] * jnp.sin(angles)], axis=0
    ).astype(BF16)

    by_slot = fetch_list.transpose(0, 2, 1)
    owner_row = lax.dynamic_index_in_dim(by_slot, position, 0, keepdims=False)
    picked = synthesize(owner_row, coeff, turns, table, fields)
    fetched = lax.all_to_all(picked, "dev", split_axis=0, concat_axis=0, tiled=True)

    taps = noise_kernel.astype(BF16).astype(F32)
    band = jnp.concatenate(
        [
            jnp.zeros((scans, 1), F32),
            taps[:, ::-1],
            taps[:, 1:],
            jnp.zeros((scans, HALF_BLK), F32),
        ],
        axis=1,
    )
    strips = band_strips(band[:, None, :])
    pix = block_pix.reshape(scans, -1, TILE)
    per_slot = scan_stage(
        scan_tiles,
        block_tile,
        scan_weight,
        fetched.reshape(-1, fields, TILE),
        pix,
        strips,
    )
    returned = lax.all_to_all(
        per_slot.reshape(fetched.shape), "dev", split_axis=0, concat_axis=0, tiled=True
    )
    return owner_sum(owner_row, returned)


def solution(mesh):
    return jax.shard_map(
        local,
        mesh=mesh,
        in_specs=(
            P("half", None),
            P("dev", None, "half", None),
            P("dev", None, None),
            P(),
            P(),
            P("dev", None),
            P("dev", None),
            P("dev", None),
            P("dev", None),
            P("dev"),
        ),
        out_specs=P("dev", "half", None),
        check_vma=False,
    )
```

```python
import math

import jax
import jax.numpy as jnp
from jax import lax
from jax.experimental import pallas as pl
from jax.experimental.pallas import tpu as pltpu
from jax.sharding import PartitionSpec as P

NPHI = 4096
TILE = 128
BLK = 512
HALF_BLK = 256
F32 = jnp.float32
BF16 = jnp.bfloat16
VMEM_LIMIT = 24 * 1024 * 1024


def cos_sin(k):
    quarter = jnp.floor(k * (1.0 / 2048.0) + 0.5)
    y = (k - 2048.0 * quarter) * (math.pi / NPHI)
    y2 = y * y
    sine = y * (1.0 + y2 * (-1.0 / 6.0 + y2 * (1.0 / 120.0 + y2 * (-1.0 / 5040.0))))
    cosine = 1.0 + y2 * (
        -0.5 + y2 * (1.0 / 24.0 + y2 * (-1.0 / 720.0 + y2 * (1.0 / 40320.0)))
    )
    turn = quarter - 4.0 * jnp.floor(quarter * 0.25)
    odd = (turn == 1.0) | (turn == 3.0)
    cos_sign = jnp.where((turn == 1.0) | (turn == 2.0), -1.0, 1.0)
    sin_sign = jnp.where(turn >= 2.0, -1.0, 1.0)
    return jnp.where(odd, sine, cosine) * cos_sign, jnp.where(odd, cosine, sine) * sin_sign


def legendre_kernel(
    ids_ref, alm_hbm, leg_hbm, out_ref, turn_ref, table_ref, alm_buf, leg_buf, sems
):
    orders, devices = ids_ref.shape
    copies = []
    for s in range(orders):
        a = pltpu.make_async_copy(alm_hbm.at[s], alm_buf.at[s], sems.at[0, s])
        b = pltpu.make_async_copy(leg_hbm.at[s], leg_buf.at[s], sems.at[1, s])
        a.start()
        b.start()
        copies.append((a, b))
    ids = ids_ref[...].astype(F32)
    tiles = turn_ref.shape[1]
    for j in range(tiles):
        turn_ref[0, j], turn_ref[1, j] = cos_sin(ids * float(j * 2 * NPHI // tiles))
    odd_pixel = (2 * lax.broadcasted_iota(jnp.int32, (devices, TILE), 1) + 1).astype(F32)
    scale = 1.0 / math.sqrt(2.0 * orders * devices)
    for s in range(orders):
        m = jnp.broadcast_to(ids[s : s + 1, :], (TILE, devices)).T
        cosine, sine = cos_sin(m * odd_pixel)
        weight = jnp.where(m == 0.0, scale, 2.0 * scale)
        table_ref[pl.ds(s * devices, devices), :] = (weight * cosine).astype(BF16)
        table_ref[pl.ds((orders + s) * devices, devices), :] = (-weight * sine).astype(BF16)
    for s in range(orders):
        copies[s][0].wait()
        copies[s][1].wait()
        rows = alm_buf.shape[1]
        out_ref[pl.ds(s * rows, rows), :] = jnp.dot(
            alm_buf[s], leg_buf[s], preferred_element_type=F32
        )


def contract_ells(ids, alm, legendre):
    orders, parts, fields, ells = alm.shape
    cycles = legendre.shape[2]
    devices = ids.shape[1]
    rows = parts * fields
    tiles = NPHI // TILE
    return pl.pallas_call(
        legendre_kernel,
        out_shape=(
            jax.ShapeDtypeStruct((orders * rows, cycles), F32),
            jax.ShapeDtypeStruct((2, tiles, orders, devices), F32),
            jax.ShapeDtypeStruct((2 * orders * devices, TILE), BF16),
        ),
        in_specs=[
            pl.BlockSpec(memory_space=pltpu.VMEM),
            pl.BlockSpec(memory_space=pl.ANY),
            pl.BlockSpec(memory_space=pl.ANY),
        ],
        scratch_shapes=[
            pltpu.VMEM((orders, rows, ells), BF16),
            pltpu.VMEM((orders, ells, cycles), BF16),
            pltpu.SemaphoreType.DMA((2, orders)),
        ],
        compiler_params=pltpu.CompilerParams(vmem_limit_bytes=VMEM_LIMIT),
        name="contract_ells",
    )(
        ids,
        pltpu.with_memory_space_constraint(alm.reshape(orders, rows, ells), pltpu.HBM),
        pltpu.with_memory_space_constraint(legendre, pltpu.HBM),
    )


def split_bf16(x):
    high = x.astype(BF16)
    return high, (x - high.astype(F32)).astype(BF16)


def mix_kernel(half_ref, own_ref, other_ref, mix_ref, out_ref):
    fields = mix_ref.shape[0]
    rows = own_ref.shape[0]
    repeats = rows // fields
    low, high = mix_ref[:, :fields], mix_ref[:, fields:]
    first = half_ref[0] == 0
    same_group = (
        lax.broadcasted_iota(jnp.int32, (rows, rows), 0) // fields
        == lax.broadcasted_iota(jnp.int32, (rows, rows), 1) // fields
    )

    def spread(mix):
        wide = jnp.concatenate([mix] * repeats, axis=1)
        wide = jnp.concatenate([wide] * repeats, axis=0)
        return split_bf16(jnp.where(same_group, wide, 0.0))

    total = None
    for mix, values in (
        (jnp.where(first, low, high), own_ref),
        (jnp.where(first, high, low), other_ref),
    ):
        mix_high, mix_low = spread(mix)
        val_high, val_low = split_bf16(values[...])
        for x, y in ((mix_high, val_high), (mix_high, val_low), (mix_low, val_high)):
            term = jnp.dot(x, y, preferred_element_type=F32)
            total = term if total is None else total + term
    by_cycle = total.T.astype(BF16)
    lanes = out_ref.shape[2]
    for p in range(out_ref.shape[1]):
        out_ref[:, p, :] = by_cycle[:, p * lanes : (p + 1) * lanes]


def mix_fields(half, own, other, field_mix):
    rows, cycles = own.shape
    vmem = pl.BlockSpec(memory_space=pltpu.VMEM)
    return pl.pallas_call(
        mix_kernel,
        out_shape=jax.ShapeDtypeStruct((cycles, rows // 128, 128), BF16),
        in_specs=[pl.BlockSpec(memory_space=pltpu.SMEM), vmem, vmem, vmem],
        compiler_params=pltpu.CompilerParams(vmem_limit_bytes=VMEM_LIMIT),
        name="mix_fields",
    )(half, own, other, field_mix)


def synth_kernel(
    position_ref,
    list_ref,
    coeff_ref,
    turn_ref,
    table_ref,
    out_ref,
    lhs_ref,
    map_ref,
    owner_ref,
    sem,
):
    row_copy = pltpu.make_async_copy(list_ref.at[position_ref[0]], owner_ref, sem)
    row_copy.start()
    devices, groups, lanes = coeff_ref.shape
    tiles, fields = map_ref.shape[0], map_ref.shape[1]
    slots = turn_ref.shape[2]
    per_group = slots // groups
    k_half = slots * devices
    flipped = [coeff_ref[:, g, :].astype(F32).T for g in range(groups)]
    for s in range(slots):
        block = flipped[s // per_group]
        at = (s % per_group) * 2 * fields
        real = block[at : at + fields]
        imag = block[at + fields : at + 2 * fields]
        for j in range(tiles):
            cos_row = turn_ref[0, j, s : s + 1, :]
            sin_row = turn_ref[1, j, s : s + 1, :]
            rows = pl.ds(j * fields, fields)
            lhs_ref[rows, pl.ds(s * devices, devices)] = (real * cos_row - imag * sin_row).astype(
                BF16
            )
            lhs_ref[rows, pl.ds(k_half + s * devices, devices)] = (
                real * sin_row + imag * cos_row
            ).astype(BF16)
    pixels = jnp.dot(lhs_ref[...], table_ref[...], preferred_element_type=F32).astype(BF16)
    map_ref[...] = pixels.reshape(tiles, fields, TILE)
    capacity = out_ref.shape[1]
    row_copy.wait()

    def pick(e, carry):
        for k in range(capacity):
            g = jnp.maximum(owner_ref[k, e], 0)
            out_ref[e, k] = map_ref[g]
        return carry

    lax.fori_loop(0, out_ref.shape[0], pick, 0, unroll=8)


def synthesize(position, by_slot, coeff, turns, table, fields):
    devices, capacity, _ = by_slot.shape
    tiles = turns.shape[1]
    k_total = table.shape[0]
    return pl.pallas_call(
        synth_kernel,
        out_shape=jax.ShapeDtypeStruct((devices, capacity, fields, TILE), BF16),
        in_specs=[
            pl.BlockSpec(memory_space=pltpu.SMEM),
            pl.BlockSpec(memory_space=pl.ANY),
            pl.BlockSpec(memory_space=pltpu.VMEM),
            pl.BlockSpec(memory_space=pltpu.VMEM),
            pl.BlockSpec(memory_space=pltpu.VMEM),
        ],
        scratch_shapes=[
            pltpu.VMEM((tiles * fields, k_total), BF16),
            pltpu.VMEM((tiles, fields, TILE), BF16),
            pltpu.SMEM((capacity, devices), jnp.int32),
            pltpu.SemaphoreType.DMA,
        ],
        compiler_params=pltpu.CompilerParams(vmem_limit_bytes=VMEM_LIMIT),
        name="synthesize",
    )(position, by_slot, coeff, turns, table)


def band_kernel(row_ref, out_ref):
    rows, width = out_ref.shape[1], out_ref.shape[2]
    wide = jnp.broadcast_to(row_ref[0], (rows, width))
    out_ref[0] = pltpu.roll(wide, 0, 1, stride=1, stride_axis=0).astype(BF16)


def band_strips(rows):
    scans, _, width = rows.shape
    return pl.pallas_call(
        band_kernel,
        grid=(scans,),
        out_shape=jax.ShapeDtypeStruct((scans, HALF_BLK, width), BF16),
        in_specs=[pl.BlockSpec((1, 1, width), lambda n: (n, 0, 0))],
        out_specs=pl.BlockSpec((1, HALF_BLK, width), lambda n: (n, 0, 0)),
        compiler_params=pltpu.CompilerParams(vmem_limit_bytes=VMEM_LIMIT),
        name="band_strips",
    )(rows)


def scan_kernel(
    list_ref, entry_ref, weight_ref, tiles_ref, pix_ref, strip_ref, out_ref, pad_ref, wtd_ref, sum_ref
):
    n = pl.program_id(0)
    fields = tiles_ref.shape[1]
    blocks = entry_ref.shape[1]
    halves = 2 * blocks
    edge = 2 * fields

    @pl.when(n == 0)
    def _():
        sum_ref[...] = jnp.zeros_like(sum_ref)
        pad_ref[pl.ds(0, edge), :] = jnp.zeros((edge, HALF_BLK), BF16)
        pad_ref[pl.ds(edge + halves * fields, edge), :] = jnp.zeros((edge, HALF_BLK), BF16)

    per_half = HALF_BLK // TILE
    quarters = BLK // TILE

    def gather(b, carry):
        slot = list_ref[n, entry_ref[n, b]]
        tile = tiles_ref[slot].astype(F32)
        for q in range(quarters):
            row = pix_ref[0, pl.ds(b * quarters + q, 1), :]
            at = jnp.broadcast_to(row, (8, TILE))
            live = at >= 0
            index = jnp.maximum(at, 0)
            parts = [
                jnp.where(
                    live,
                    jnp.take_along_axis(
                        tile[8 * i : 8 * i + 8], index, axis=1, mode="promise_in_bounds"
                    ),
                    0.0,
                )
                for i in range(fields // 8)
            ]
            start = pl.multiple_of(edge + (2 * b + q // per_half) * fields, fields)
            pad_ref[pl.ds(start, fields), pl.ds((q % per_half) * TILE, TILE)] = jnp.concatenate(
                parts, axis=0
            ).astype(BF16)
        return carry

    lax.fori_loop(0, blocks, gather, 0, unroll=16)
    total = None
    for d in range(-2, 3):
        term = jnp.dot(
            pad_ref[pl.ds(edge - d * fields, halves * fields), :],
            strip_ref[0, :, pl.ds((d + 2) * HALF_BLK, HALF_BLK)],
            preferred_element_type=F32,
        )
        total = term if total is None else total + term
    wtd_ref[...] = (weight_ref[n] * total).astype(BF16)
    packed = 16
    pixel_iota = lax.broadcasted_iota(jnp.int32, (TILE, TILE), 0).astype(F32).astype(BF16)
    one, zero = jnp.asarray(1, BF16), jnp.asarray(0, BF16)

    def one_hot(b, q):
        row = pix_ref[0, pl.ds(b * quarters + q, 1), :]
        row = jnp.broadcast_to(row, (packed, TILE)).astype(F32).astype(BF16)
        return jnp.where(pixel_iota == jnp.concatenate([row] * (TILE // packed), axis=0), one, zero)

    def bin_block(b, carry):
        slot = list_ref[n, entry_ref[n, b]]
        hot = jnp.concatenate([one_hot(b, q) for q in range(quarters)], axis=1)
        start = pl.multiple_of(2 * b * fields, fields)
        values = jnp.concatenate(
            [wtd_ref[pl.ds(start + h * fields, fields), :] for h in range(2)], axis=1
        )
        partial = lax.dot_general(
            values, hot, (((1,), (1,)), ((), ())), preferred_element_type=F32
        )
        sum_ref[slot] = sum_ref[slot] + partial
        return carry

    lax.fori_loop(0, blocks, bin_block, 0, unroll=16)

    @pl.when(n == pl.num_programs(0) - 1)
    def _():
        out_ref[...] = sum_ref[...].astype(BF16)


def scan_stage(scan_tiles, block_tile, scan_weight, tiles, pix, strips):
    slots, fields, _ = tiles.shape
    scans, blocks = block_tile.shape
    rows = blocks * BLK // TILE
    width = strips.shape[2]
    smem = pl.BlockSpec(memory_space=pltpu.SMEM)
    whole = pl.BlockSpec((slots, fields, TILE), lambda n: (0, 0, 0))
    return pl.pallas_call(
        scan_kernel,
        grid=(scans,),
        out_shape=jax.ShapeDtypeStruct((slots, fields, TILE), BF16),
        in_specs=[
            smem,
            smem,
            smem,
            whole,
            pl.BlockSpec((1, rows, TILE), lambda n: (n, 0, 0)),
            pl.BlockSpec((1, HALF_BLK, width), lambda n: (n, 0, 0)),
        ],
        out_specs=whole,
        scratch_shapes=[
            pltpu.VMEM(((2 * blocks + 4) * fields, HALF_BLK), BF16),
            pltpu.VMEM((2 * blocks * fields, HALF_BLK), BF16),
            pltpu.VMEM((slots, fields, TILE), F32),
        ],
        compiler_params=pltpu.CompilerParams(
            vmem_limit_bytes=VMEM_LIMIT, dimension_semantics=("arbitrary",)
        ),
        name="scan_stage",
    )(scan_tiles, block_tile, scan_weight, tiles, pix, strips)


def owner_kernel(position_ref, list_ref, back_ref, out_ref, owner_ref, sem, *sum_refs):
    row_copy = pltpu.make_async_copy(list_ref.at[position_ref[0]], owner_ref, sem)
    row_copy.start()
    capacity, devices = owner_ref.shape
    tiles = sum_refs[0].shape[0] - 1
    lanes = len(sum_refs) // capacity
    for ref in sum_refs:
        ref[...] = jnp.zeros_like(ref)
    row_copy.wait()

    def add(i, carry):
        for j in range(lanes):
            e = i * lanes + j
            for k in range(capacity):
                ref = sum_refs[j * capacity + k]
                g = owner_ref[k, e]
                g = jnp.where(g < 0, tiles, g)
                ref[g] = ref[g] + back_ref[e, k].astype(F32)
        return carry

    lax.fori_loop(0, devices // lanes, add, 0, unroll=8)
    for g in range(tiles):
        total = sum_refs[0][g]
        for ref in sum_refs[1:]:
            total = total + ref[g]
        out_ref[0, :, pl.ds(g * TILE, TILE)] = total


def owner_sum(position, by_slot, returned):
    devices, capacity, fields, _ = returned.shape
    tiles = NPHI // TILE
    return pl.pallas_call(
        owner_kernel,
        out_shape=jax.ShapeDtypeStruct((1, fields, NPHI), F32),
        in_specs=[
            pl.BlockSpec(memory_space=pltpu.SMEM),
            pl.BlockSpec(memory_space=pl.ANY),
            pl.BlockSpec(memory_space=pltpu.VMEM),
        ],
        scratch_shapes=[
            pltpu.SMEM((capacity, devices), jnp.int32),
            pltpu.SemaphoreType.DMA,
        ]
        + [pltpu.VMEM((tiles + 1, fields, TILE), F32)] * (2 * capacity),
        compiler_params=pltpu.CompilerParams(vmem_limit_bytes=VMEM_LIMIT),
        name="owner_sum",
    )(position, by_slot, returned)


def local(
    field_mix,
    alm,
    legendre,
    order_ids,
    fetch_list,
    scan_tiles,
    block_tile,
    block_pix,
    noise_kernel,
    scan_weight,
):
    half = lax.axis_index("half").reshape(1)
    position = lax.axis_index("dev").reshape(1)
    devices = fetch_list.shape[0]
    fields = alm.shape[2]
    slots = alm.shape[0]
    scans = block_pix.shape[0]

    ids = order_ids.reshape(devices, slots).T
    own, turns, table = contract_ells(ids, alm, legendre)
    other = lax.ppermute(own, "half", [(0, 1), (1, 0)])
    sent = mix_fields(half, own, other, field_mix)
    coeff = lax.all_to_all(sent, "dev", split_axis=0, concat_axis=0, tiled=True)

    by_slot = fetch_list.transpose(0, 2, 1)
    picked = synthesize(position, by_slot, coeff, turns, table, fields)
    picked, noise_kernel, block_pix = lax.optimization_barrier((picked, noise_kernel, block_pix))
    fetched = lax.all_to_all(picked, "dev", split_axis=0, concat_axis=0, tiled=True)

    taps = noise_kernel.astype(BF16).astype(F32)
    band = jnp.concatenate(
        [
            jnp.zeros((scans, 1), F32),
            taps[:, ::-1],
            taps[:, 1:],
            jnp.zeros((scans, HALF_BLK), F32),
        ],
        axis=1,
    )
    strips = band_strips(band[:, None, :])
    pix = block_pix.reshape(scans, -1, TILE)
    per_slot = scan_stage(
        scan_tiles,
        block_tile,
        scan_weight,
        fetched.reshape(-1, fields, TILE),
        pix,
        strips,
    )
    returned = lax.all_to_all(
        per_slot.reshape(fetched.shape), "dev", split_axis=0, concat_axis=0, tiled=True
    )
    return owner_sum(position, by_slot, returned)


def solution(mesh):
    return jax.shard_map(
        local,
        mesh=mesh,
        in_specs=(
            P("half", None),
            P("dev", None, "half", None),
            P("dev", None, None),
            P(),
            P(),
            P("dev", None),
            P("dev", None),
            P("dev", None),
            P("dev", None),
            P("dev"),
        ),
        out_specs=P("dev", "half", None),
        check_vma=False,
    )
```

```python
import math

import jax
import jax.numpy as jnp
from jax import lax
from jax.experimental import pallas as pl
from jax.experimental.pallas import tpu as pltpu
from jax.sharding import PartitionSpec as P

NPHI = 4096
TILE = 128
BLK = 512
HALF_BLK = 256
RING = 8
SHARE = 2
COPIES = RING // SHARE
F32 = jnp.float32
BF16 = jnp.bfloat16
VMEM_LIMIT = 24 * 1024 * 1024
SCAN_LIMIT = 40 * 1024 * 1024


def cos_sin(k):
    quarter = jnp.floor(k * (1.0 / 2048.0) + 0.5)
    y = (k - 2048.0 * quarter) * (math.pi / NPHI)
    y2 = y * y
    sine = y * (1.0 + y2 * (-1.0 / 6.0 + y2 * (1.0 / 120.0 + y2 * (-1.0 / 5040.0))))
    cosine = 1.0 + y2 * (
        -0.5 + y2 * (1.0 / 24.0 + y2 * (-1.0 / 720.0 + y2 * (1.0 / 40320.0)))
    )
    turn = quarter - 4.0 * jnp.floor(quarter * 0.25)
    odd = (turn == 1.0) | (turn == 3.0)
    cos_sign = jnp.where((turn == 1.0) | (turn == 2.0), -1.0, 1.0)
    sin_sign = jnp.where(turn >= 2.0, -1.0, 1.0)
    return jnp.where(odd, sine, cosine) * cos_sign, jnp.where(odd, cosine, sine) * sin_sign


def legendre_kernel(
    ids_ref, alm_hbm, leg_hbm, out_ref, turn_ref, table_ref, alm_buf, leg_buf, sems
):
    orders, devices = turn_ref.shape[2:]
    copies = []
    for s in range(orders):
        a = pltpu.make_async_copy(alm_hbm.at[s], alm_buf.at[s], sems.at[0, s])
        b = pltpu.make_async_copy(leg_hbm.at[s], leg_buf.at[s], sems.at[1, s])
        a.start()
        b.start()
        copies.append((a, b))
    flat = ids_ref[...].astype(F32)
    lane = lax.broadcasted_iota(jnp.int32, (orders, TILE), 1)
    slot = lax.broadcasted_iota(jnp.int32, (orders, TILE), 0)
    spread = jnp.concatenate(
        [jnp.where(lane % orders == slot, flat[i : i + 1, :], 0.0) for i in range(flat.shape[0])],
        axis=1,
    )
    count = orders * devices
    holder = (
        lax.broadcasted_iota(jnp.int32, (count, devices), 0) // orders
        == lax.broadcasted_iota(jnp.int32, (count, devices), 1)
    ).astype(F32).astype(BF16)
    ids = sum(
        jnp.dot(part, holder, preferred_element_type=F32) for part in split_bf16(spread)
    )
    tiles = turn_ref.shape[1]
    for j in range(tiles):
        turn_ref[0, j], turn_ref[1, j] = cos_sin(ids * float(j * 2 * NPHI // tiles))
    odd_pixel = (2 * lax.broadcasted_iota(jnp.int32, (devices, TILE), 1) + 1).astype(F32)
    scale = 1.0 / math.sqrt(2.0 * orders * devices)
    for s in range(orders):
        m = jnp.broadcast_to(ids[s : s + 1, :], (TILE, devices)).T
        cosine, sine = cos_sin(m * odd_pixel)
        weight = jnp.where(m == 0.0, scale, 2.0 * scale)
        table_ref[pl.ds(s * devices, devices), :] = (weight * cosine).astype(BF16)
        table_ref[pl.ds((orders + s) * devices, devices), :] = (-weight * sine).astype(BF16)
    for s in range(orders):
        copies[s][0].wait()
        copies[s][1].wait()
        rows = alm_buf.shape[1]
        out_ref[pl.ds(s * rows, rows), :] = jnp.dot(
            alm_buf[s], leg_buf[s], preferred_element_type=F32
        )


def contract_ells(ids, alm, legendre):
    orders, parts, fields, ells = alm.shape
    cycles = legendre.shape[2]
    devices = ids.shape[0] // orders
    rows = parts * fields
    tiles = NPHI // TILE
    return pl.pallas_call(
        legendre_kernel,
        out_shape=(
            jax.ShapeDtypeStruct((orders * rows, cycles), F32),
            jax.ShapeDtypeStruct((2, tiles, orders, devices), F32),
            jax.ShapeDtypeStruct((2 * orders * devices, TILE), BF16),
        ),
        in_specs=[
            pl.BlockSpec(memory_space=pltpu.VMEM),
            pl.BlockSpec(memory_space=pl.ANY),
            pl.BlockSpec(memory_space=pl.ANY),
        ],
        scratch_shapes=[
            pltpu.VMEM((orders, rows, ells), BF16),
            pltpu.VMEM((orders, ells, cycles), BF16),
            pltpu.SemaphoreType.DMA((2, orders)),
        ],
        compiler_params=pltpu.CompilerParams(vmem_limit_bytes=VMEM_LIMIT),
        name="contract_ells",
    )(
        ids.reshape(-1, TILE),
        pltpu.with_memory_space_constraint(alm.reshape(orders, rows, ells), pltpu.HBM),
        pltpu.with_memory_space_constraint(legendre, pltpu.HBM),
    )


def split_bf16(x):
    high = x.astype(BF16)
    return high, (x - high.astype(F32)).astype(BF16)


def mix_kernel(half_ref, own_ref, other_ref, mix_ref, out_ref):
    fields = mix_ref.shape[0]
    rows = own_ref.shape[0]
    repeats = rows // fields
    low, high = mix_ref[:, :fields], mix_ref[:, fields:]
    first = half_ref[0] == 0
    same_group = (
        lax.broadcasted_iota(jnp.int32, (rows, rows), 0) // fields
        == lax.broadcasted_iota(jnp.int32, (rows, rows), 1) // fields
    )

    def spread(mix):
        wide = jnp.concatenate([mix] * repeats, axis=1)
        wide = jnp.concatenate([wide] * repeats, axis=0)
        return split_bf16(jnp.where(same_group, wide, 0.0))

    total = None
    for mix, values in (
        (jnp.where(first, low, high), own_ref),
        (jnp.where(first, high, low), other_ref),
    ):
        mix_high, mix_low = spread(mix)
        val_high, val_low = split_bf16(values[...])
        for x, y in ((mix_high, val_high), (mix_high, val_low), (mix_low, val_high)):
            term = jnp.dot(x, y, preferred_element_type=F32)
            total = term if total is None else total + term
    rounded = total.astype(BF16)
    lanes = out_ref.shape[2]
    cycles = total.shape[1]
    parts = rows // lanes
    per_target = parts * COPIES
    count = out_ref.shape[0] * per_target
    row = lax.broadcasted_iota(jnp.int32, (count, cycles), 0)
    target, inner = row // per_target, row % per_target
    cycle = (target // RING) * RING + target % SHARE + SHARE * (inner % COPIES)
    wanted = cycle == lax.broadcasted_iota(jnp.int32, (count, cycles), 1)
    spread_out = None
    for p in range(parts):
        pick = (wanted & (inner // COPIES == p)).astype(F32).astype(BF16)
        term = lax.dot_general(
            pick,
            rounded[p * lanes : (p + 1) * lanes],
            (((1,), (1,)), ((), ())),
            preferred_element_type=F32,
        )
        spread_out = term if spread_out is None else spread_out + term
    out_ref[...] = spread_out.reshape(out_ref.shape).astype(BF16)


def mix_fields(half, own, other, field_mix):
    rows, cycles = own.shape
    vmem = pl.BlockSpec(memory_space=pltpu.VMEM)
    return pl.pallas_call(
        mix_kernel,
        out_shape=jax.ShapeDtypeStruct((cycles, rows // TILE * COPIES, TILE), BF16),
        in_specs=[pl.BlockSpec(memory_space=pltpu.SMEM), vmem, vmem, vmem],
        compiler_params=pltpu.CompilerParams(vmem_limit_bytes=VMEM_LIMIT),
        name="mix_fields",
    )(half, own, other, field_mix)


def synth_kernel(
    position_ref,
    list_ref,
    coeff_ref,
    turn_ref,
    table_ref,
    out_ref,
    flip_ref,
    even_ref,
    odd_ref,
    map_ref,
    owner_ref,
    sems,
):
    position = position_ref[0]
    ring_at = position % RING
    first = position - ring_at + ring_at % SHARE
    row_copies = [
        pltpu.make_async_copy(list_ref.at[first + SHARE * k], owner_ref.at[k], sems.at[k])
        for k in range(COPIES)
    ]
    for copy in row_copies:
        copy.start()
    devices = coeff_ref.shape[0]
    groups = coeff_ref.shape[1] // COPIES
    tiles, fields = map_ref.shape[1:3]
    slots = turn_ref.shape[2]
    per_group = slots // groups
    k_half = slots * devices
    for k in range(COPIES):
        for g in range(groups):
            flip_ref[k, g] = coeff_ref[:, g * COPIES + k, :].astype(F32).T

    def one_cycle(k, lhs):
        for s in range(slots):
            at = (s % per_group) * 2 * fields
            real = flip_ref[k, s // per_group, pl.ds(at, fields), :]
            imag = flip_ref[k, s // per_group, pl.ds(at + fields, fields), :]
            for j in range(tiles):
                cos_row = turn_ref[0, j, s : s + 1, :]
                sin_row = turn_ref[1, j, s : s + 1, :]
                rows = pl.ds(j * fields, fields)
                lhs[rows, pl.ds(s * devices, devices)] = (
                    real * cos_row - imag * sin_row
                ).astype(BF16)
                lhs[rows, pl.ds(k_half + s * devices, devices)] = (
                    real * sin_row + imag * cos_row
                ).astype(BF16)
        pixels = jnp.dot(lhs[...], table_ref[...], preferred_element_type=F32).astype(BF16)
        map_ref[k] = pixels.reshape(tiles, fields, TILE)

    def cycle_pair(i, carry):
        for u, lhs in enumerate((even_ref, odd_ref)):
            one_cycle(2 * i + u, lhs)
        return carry

    lax.fori_loop(0, COPIES // 2, cycle_pair, 0)
    for copy in row_copies:
        copy.wait()
    capacity = out_ref.shape[2]
    base = ring_at - ring_at % SHARE

    def pick(t, carry):
        e = (t // SHARE) * RING + base + t % SHARE
        for k in range(COPIES):
            for c in range(capacity):
                out_ref[t, k, c] = map_ref[k, jnp.maximum(owner_ref[k, c, e], 0)]
        return carry

    lax.fori_loop(0, out_ref.shape[0], pick, 0, unroll=2)


def synthesize(position, by_slot, coeff, turns, table, fields):
    devices, capacity, _ = by_slot.shape
    tiles = turns.shape[1]
    k_total = table.shape[0]
    groups = coeff.shape[1] // COPIES
    vmem = pl.BlockSpec(memory_space=pltpu.VMEM)
    return pl.pallas_call(
        synth_kernel,
        out_shape=jax.ShapeDtypeStruct(
            (devices // COPIES, COPIES, capacity, fields, TILE), BF16
        ),
        in_specs=[
            pl.BlockSpec(memory_space=pltpu.SMEM),
            pl.BlockSpec(memory_space=pl.ANY),
            vmem,
            vmem,
            vmem,
        ],
        scratch_shapes=[
            pltpu.VMEM((COPIES, groups, TILE, devices), F32),
            pltpu.VMEM((tiles * fields, k_total), BF16),
            pltpu.VMEM((tiles * fields, k_total), BF16),
            pltpu.VMEM((COPIES, tiles, fields, TILE), BF16),
            pltpu.SMEM((COPIES, capacity, devices), jnp.int32),
            pltpu.SemaphoreType.DMA((COPIES,)),
        ],
        compiler_params=pltpu.CompilerParams(vmem_limit_bytes=VMEM_LIMIT),
        name="synthesize",
    )(position, by_slot, coeff, turns, table)


def band_kernel(row_ref, out_ref):
    rows, width = out_ref.shape[1], out_ref.shape[2]
    wide = jnp.broadcast_to(row_ref[0], (rows, width))
    out_ref[0] = pltpu.roll(wide, 0, 1, stride=1, stride_axis=0).astype(BF16)


def band_strips(rows):
    scans, _, width = rows.shape
    return pl.pallas_call(
        band_kernel,
        grid=(scans,),
        out_shape=jax.ShapeDtypeStruct((scans, HALF_BLK, width), BF16),
        in_specs=[pl.BlockSpec((1, 1, width), lambda n: (n, 0, 0))],
        out_specs=pl.BlockSpec((1, HALF_BLK, width), lambda n: (n, 0, 0)),
        compiler_params=pltpu.CompilerParams(vmem_limit_bytes=VMEM_LIMIT),
        name="band_strips",
    )(rows)


def one_hot(row):
    packed = 16
    iota = lax.broadcasted_iota(jnp.int32, (TILE, TILE), 0).astype(F32).astype(BF16)
    row = jnp.broadcast_to(row, (packed, TILE)).astype(F32).astype(BF16)
    row = jnp.concatenate([row] * (TILE // packed), axis=0)
    return jnp.where(iota == row, jnp.asarray(1, BF16), jnp.asarray(0, BF16))


def hot_kernel(pix_ref, out_ref):
    quarters = BLK // TILE

    def body(b, carry):
        for q in range(quarters):
            row = pix_ref[0, pl.ds(b * quarters + q, 1), :]
            out_ref[0, b, pl.ds(q * TILE, TILE), :] = one_hot(row).T
        return carry

    lax.fori_loop(0, out_ref.shape[1], body, 0, unroll=8)


def hot_blocks(pix):
    scans, rows, _ = pix.shape
    blocks = rows * TILE // BLK
    hots = pl.pallas_call(
        hot_kernel,
        grid=(scans,),
        out_shape=jax.ShapeDtypeStruct((scans, blocks, BLK, TILE), BF16),
        in_specs=[pl.BlockSpec((1, rows, TILE), lambda n: (n, 0, 0))],
        out_specs=pl.BlockSpec((1, blocks, BLK, TILE), lambda n: (n, 0, 0, 0)),
        compiler_params=pltpu.CompilerParams(vmem_limit_bytes=VMEM_LIMIT),
        name="hot_blocks",
    )(pix)
    return pltpu.with_memory_space_constraint(hots, pltpu.HBM)


def scan_kernel(
    list_ref,
    moved_ref,
    entry_ref,
    weight_ref,
    tiles_ref,
    pix_ref,
    strip_ref,
    hot_hbm,
    out_ref,
    pad_ref,
    wtd_ref,
    sum_ref,
    hot_ref,
    sems,
):
    scans, blocks = entry_ref.shape
    copies = [
        pltpu.make_async_copy(hot_hbm.at[n], hot_ref.at[n], sems.at[n]) for n in range(scans)
    ]
    for copy in copies:
        copy.start()
    fields = tiles_ref.shape[1]
    halves = 2 * blocks
    edge = 2 * fields
    per_half = HALF_BLK // TILE
    quarters = BLK // TILE
    sum_ref[...] = jnp.zeros_like(sum_ref)
    for p in range(2):
        pad_ref[p, pl.ds(0, edge), :] = jnp.zeros((edge, HALF_BLK), BF16)
        pad_ref[p, pl.ds(edge + halves * fields, edge), :] = jnp.zeros((edge, HALF_BLK), BF16)

    def gather(n, b):
        tile = tiles_ref[moved_ref[n, entry_ref[n, b]]].astype(F32)
        for q in range(quarters):
            at = jnp.broadcast_to(pix_ref[n, pl.ds(b * quarters + q, 1), :], (8, TILE))
            live = at >= 0
            index = jnp.maximum(at, 0)
            parts = [
                jnp.where(
                    live,
                    jnp.take_along_axis(
                        tile[8 * i : 8 * i + 8], index, axis=1, mode="promise_in_bounds"
                    ),
                    0.0,
                )
                for i in range(fields // 8)
            ]
            start = pl.multiple_of(edge + (2 * b + q // per_half) * fields, fields)
            pad_ref[
                n % 2, pl.ds(start, fields), pl.ds((q % per_half) * TILE, TILE)
            ] = jnp.concatenate(parts, axis=0).astype(BF16)

    def filter_scan(n):
        total = None
        for d in range(-2, 3):
            term = jnp.dot(
                pad_ref[n % 2, pl.ds(edge - d * fields, halves * fields), :],
                strip_ref[n, :, pl.ds((d + 2) * HALF_BLK, HALF_BLK)],
                preferred_element_type=F32,
            )
            total = term if total is None else total + term
        wtd_ref[...] = (weight_ref[n] * total).astype(BF16)

    def bin_block(n, b):
        slot = list_ref[n, entry_ref[n, b]]
        start = pl.multiple_of(2 * b * fields, fields)
        values = jnp.concatenate(
            [wtd_ref[pl.ds(start + h * fields, fields), :] for h in range(2)], axis=1
        )
        sum_ref[slot] = sum_ref[slot] + jnp.dot(
            values, hot_ref[n, b], preferred_element_type=F32
        )

    def run(body):
        lax.fori_loop(0, blocks, lambda b, carry: (body(b), carry)[1], 0, unroll=16)

    run(lambda b: gather(0, b))
    for n in range(scans):
        filter_scan(n)
        copies[n].wait()

        def both(b, n=n):
            bin_block(n, b)
            if n + 1 < scans:
                gather(n + 1, b)

        run(both)
    out_ref[...] = sum_ref[...].astype(BF16)


def scan_stage(scan_tiles, moved, block_tile, scan_weight, tiles, pix, strips, hots):
    slots, fields, _ = tiles.shape
    blocks = block_tile.shape[1]
    smem = pl.BlockSpec(memory_space=pltpu.SMEM)
    vmem = pl.BlockSpec(memory_space=pltpu.VMEM)
    return pl.pallas_call(
        scan_kernel,
        out_shape=jax.ShapeDtypeStruct((slots, fields, TILE), BF16),
        in_specs=[smem, smem, smem, smem, vmem, vmem, vmem, pl.BlockSpec(memory_space=pl.ANY)],
        out_specs=vmem,
        scratch_shapes=[
            pltpu.VMEM((2, (2 * blocks + 4) * fields, HALF_BLK), BF16),
            pltpu.VMEM((2 * blocks * fields, HALF_BLK), BF16),
            pltpu.VMEM((slots, fields, TILE), F32),
            pltpu.VMEM(hots.shape, BF16),
            pltpu.SemaphoreType.DMA((hots.shape[0],)),
        ],
        compiler_params=pltpu.CompilerParams(vmem_limit_bytes=SCAN_LIMIT),
        name="scan_stage",
    )(scan_tiles, moved, block_tile, scan_weight, tiles, pix, strips, hots)


def owner_kernel(position_ref, list_ref, back_ref, out_ref, owner_ref, sem, *sum_refs):
    row_copy = pltpu.make_async_copy(list_ref.at[position_ref[0]], owner_ref, sem)
    row_copy.start()
    capacity, devices = owner_ref.shape
    tiles = sum_refs[0].shape[0] - 1
    lanes = len(sum_refs) // capacity
    for ref in sum_refs:
        ref[...] = jnp.zeros_like(ref)
    row_copy.wait()

    def add(i, carry):
        for j in range(lanes):
            e = i * lanes + j
            for k in range(capacity):
                ref = sum_refs[j * capacity + k]
                g = owner_ref[k, e]
                g = jnp.where(g < 0, tiles, g)
                ref[g] = ref[g] + back_ref[e, k].astype(F32)
        return carry

    lax.fori_loop(0, devices // lanes, add, 0, unroll=8)
    for g in range(tiles):
        total = sum_refs[0][g]
        for ref in sum_refs[1:]:
            total = total + ref[g]
        out_ref[0, :, pl.ds(g * TILE, TILE)] = total


def owner_sum(position, by_slot, returned):
    devices, capacity, fields, _ = returned.shape
    tiles = NPHI // TILE
    return pl.pallas_call(
        owner_kernel,
        out_shape=jax.ShapeDtypeStruct((1, fields, NPHI), F32),
        in_specs=[
            pl.BlockSpec(memory_space=pltpu.SMEM),
            pl.BlockSpec(memory_space=pl.ANY),
            pl.BlockSpec(memory_space=pltpu.VMEM),
        ],
        scratch_shapes=[
            pltpu.SMEM((capacity, devices), jnp.int32),
            pltpu.SemaphoreType.DMA,
        ]
        + [pltpu.VMEM((tiles + 1, fields, TILE), F32)] * (2 * capacity),
        compiler_params=pltpu.CompilerParams(vmem_limit_bytes=VMEM_LIMIT),
        name="owner_sum",
    )(position, by_slot, returned)


def local(
    field_mix,
    alm,
    legendre,
    order_ids,
    fetch_list,
    scan_tiles,
    block_tile,
    block_pix,
    noise_kernel,
    scan_weight,
):
    half = lax.axis_index("half").reshape(1)
    position = lax.axis_index("dev").reshape(1)
    fields = alm.shape[2]
    scans = block_pix.shape[0]

    own, turns, table = contract_ells(order_ids, alm, legendre)
    other = lax.ppermute(own, "half", [(0, 1), (1, 0)])
    sent = mix_fields(half, own, other, field_mix)
    sent, block_pix, scan_tiles = lax.optimization_barrier((sent, block_pix, scan_tiles))
    coeff = lax.all_to_all(sent, "dev", split_axis=0, concat_axis=0, tiled=True)
    pix = block_pix.reshape(scans, -1, TILE)
    hots = hot_blocks(pix)
    devices, capacity = fetch_list.shape[1:]
    source, slot = scan_tiles // capacity, scan_tiles % capacity
    member = (source // RING) * SHARE + source % SHARE
    moved = (member * COPIES + (source % RING) // SHARE) * capacity + slot

    by_slot = fetch_list.transpose(0, 2, 1)
    picked = synthesize(position, by_slot, coeff, turns, table, fields)
    picked, noise_kernel = lax.optimization_barrier((picked, noise_kernel))
    groups = [
        [RING * q + SHARE * p + i for q in range(fetch_list.shape[0] // RING) for i in range(SHARE)]
        for p in range(COPIES)
    ]
    fetched = lax.all_to_all(
        picked, "dev", split_axis=0, concat_axis=0, tiled=True, axis_index_groups=groups
    )

    taps = noise_kernel.astype(BF16).astype(F32)
    band = jnp.concatenate(
        [
            jnp.zeros((scans, 1), F32),
            taps[:, ::-1],
            taps[:, 1:],
            jnp.zeros((scans, HALF_BLK), F32),
        ],
        axis=1,
    )
    strips = band_strips(band[:, None, :])
    per_slot = scan_stage(
        scan_tiles,
        moved,
        block_tile,
        scan_weight,
        fetched.reshape(-1, fields, TILE),
        pix,
        strips,
        hots,
    )
    returned = lax.all_to_all(
        per_slot.reshape(devices, capacity, fields, TILE), "dev", split_axis=0, concat_axis=0, tiled=True
    )
    return owner_sum(position, by_slot, returned)


def solution(mesh):
    return jax.shard_map(
        local,
        mesh=mesh,
        in_specs=(
            P("half", None),
            P("dev", None, "half", None),
            P("dev", None, None),
            P(),
            P(),
            P("dev", None),
            P("dev", None),
            P("dev", None),
            P("dev", None),
            P("dev"),
        ),
        out_specs=P("dev", "half", None),
        check_vma=False,
    )
```

```python
import math

import jax
import jax.numpy as jnp
from jax import lax
from jax.experimental import pallas as pl
from jax.experimental.pallas import tpu as pltpu
from jax.sharding import PartitionSpec as P

NPHI = 4096
TILE = 128
BLK = 512
HALF_BLK = 256
RING = 8
SHARE = 2
COPIES = RING // SHARE
F32 = jnp.float32
BF16 = jnp.bfloat16
VMEM_LIMIT = 24 * 1024 * 1024
SCAN_LIMIT = 40 * 1024 * 1024


def cos_sin(k):
    quarter = jnp.floor(k * (1.0 / 2048.0) + 0.5)
    y = (k - 2048.0 * quarter) * (math.pi / NPHI)
    y2 = y * y
    sine = y * (1.0 + y2 * (-1.0 / 6.0 + y2 * (1.0 / 120.0 + y2 * (-1.0 / 5040.0))))
    cosine = 1.0 + y2 * (
        -0.5 + y2 * (1.0 / 24.0 + y2 * (-1.0 / 720.0 + y2 * (1.0 / 40320.0)))
    )
    turn = quarter - 4.0 * jnp.floor(quarter * 0.25)
    odd = (turn == 1.0) | (turn == 3.0)
    cos_sign = jnp.where((turn == 1.0) | (turn == 2.0), -1.0, 1.0)
    sin_sign = jnp.where(turn >= 2.0, -1.0, 1.0)
    return jnp.where(odd, sine, cosine) * cos_sign, jnp.where(odd, cosine, sine) * sin_sign


def legendre_kernel(
    ids_ref, alm_hbm, leg_hbm, out_ref, turn_ref, table_ref, alm_buf, leg_buf, sems
):
    orders, devices = turn_ref.shape[2:]
    copies = []
    for s in range(orders):
        a = pltpu.make_async_copy(alm_hbm.at[s], alm_buf.at[s], sems.at[0, s])
        b = pltpu.make_async_copy(leg_hbm.at[s], leg_buf.at[s], sems.at[1, s])
        a.start()
        b.start()
        copies.append((a, b))
    flat = ids_ref[...].astype(F32)
    lane = lax.broadcasted_iota(jnp.int32, (orders, TILE), 1)
    slot = lax.broadcasted_iota(jnp.int32, (orders, TILE), 0)
    spread = jnp.concatenate(
        [jnp.where(lane % orders == slot, flat[i : i + 1, :], 0.0) for i in range(flat.shape[0])],
        axis=1,
    )
    count = orders * devices
    holder = (
        lax.broadcasted_iota(jnp.int32, (count, devices), 0) // orders
        == lax.broadcasted_iota(jnp.int32, (count, devices), 1)
    ).astype(F32).astype(BF16)
    ids = sum(
        jnp.dot(part, holder, preferred_element_type=F32) for part in split_bf16(spread)
    )
    tiles = turn_ref.shape[1]
    for j in range(tiles):
        turn_ref[0, j], turn_ref[1, j] = cos_sin(ids * float(j * 2 * NPHI // tiles))
    odd_pixel = (2 * lax.broadcasted_iota(jnp.int32, (devices, TILE), 1) + 1).astype(F32)
    scale = 1.0 / math.sqrt(2.0 * orders * devices)
    for s in range(orders):
        m = jnp.broadcast_to(ids[s : s + 1, :], (TILE, devices)).T
        cosine, sine = cos_sin(m * odd_pixel)
        weight = jnp.where(m == 0.0, scale, 2.0 * scale)
        table_ref[pl.ds(s * devices, devices), :] = (weight * cosine).astype(BF16)
        table_ref[pl.ds((orders + s) * devices, devices), :] = (-weight * sine).astype(BF16)
    for s in range(orders):
        copies[s][0].wait()
        copies[s][1].wait()
        rows = alm_buf.shape[1]
        out_ref[pl.ds(s * rows, rows), :] = jnp.dot(
            alm_buf[s], leg_buf[s], preferred_element_type=F32
        )


def contract_ells(ids, alm, legendre):
    orders, parts, fields, ells = alm.shape
    cycles = legendre.shape[2]
    devices = ids.shape[0] // orders
    rows = parts * fields
    tiles = NPHI // TILE
    return pl.pallas_call(
        legendre_kernel,
        out_shape=(
            jax.ShapeDtypeStruct((orders * rows, cycles), F32),
            jax.ShapeDtypeStruct((2, tiles, orders, devices), F32),
            jax.ShapeDtypeStruct((2 * orders * devices, TILE), BF16),
        ),
        in_specs=[
            pl.BlockSpec(memory_space=pltpu.VMEM),
            pl.BlockSpec(memory_space=pl.ANY),
            pl.BlockSpec(memory_space=pl.ANY),
        ],
        scratch_shapes=[
            pltpu.VMEM((orders, rows, ells), BF16),
            pltpu.VMEM((orders, ells, cycles), BF16),
            pltpu.SemaphoreType.DMA((2, orders)),
        ],
        compiler_params=pltpu.CompilerParams(vmem_limit_bytes=VMEM_LIMIT),
        name="contract_ells",
    )(
        ids.reshape(-1, TILE),
        pltpu.with_memory_space_constraint(alm.reshape(orders, rows, ells), pltpu.HBM),
        pltpu.with_memory_space_constraint(legendre, pltpu.HBM),
    )


def split_bf16(x):
    high = x.astype(BF16)
    return high, (x - high.astype(F32)).astype(BF16)


def mix_kernel(half_ref, own_ref, other_ref, mix_ref, out_ref):
    fields = mix_ref.shape[0]
    rows = own_ref.shape[0]
    repeats = rows // fields
    low, high = mix_ref[:, :fields], mix_ref[:, fields:]
    first = half_ref[0] == 0
    same_group = (
        lax.broadcasted_iota(jnp.int32, (rows, rows), 0) // fields
        == lax.broadcasted_iota(jnp.int32, (rows, rows), 1) // fields
    )

    def spread(mix):
        wide = jnp.concatenate([mix] * repeats, axis=1)
        wide = jnp.concatenate([wide] * repeats, axis=0)
        return split_bf16(jnp.where(same_group, wide, 0.0))

    total = None
    for mix, values in (
        (jnp.where(first, low, high), own_ref),
        (jnp.where(first, high, low), other_ref),
    ):
        mix_high, mix_low = spread(mix)
        val_high, val_low = split_bf16(values[...])
        for x, y in ((mix_high, val_high), (mix_high, val_low), (mix_low, val_high)):
            term = jnp.dot(x, y, preferred_element_type=F32)
            total = term if total is None else total + term
    rounded = total.astype(BF16)
    lanes = out_ref.shape[2]
    cycles = total.shape[1]
    parts = rows // lanes
    per_target = parts * COPIES
    count = out_ref.shape[0] * per_target
    row = lax.broadcasted_iota(jnp.int32, (count, cycles), 0)
    target, inner = row // per_target, row % per_target
    cycle = (target // RING) * RING + target % SHARE + SHARE * (inner % COPIES)
    wanted = cycle == lax.broadcasted_iota(jnp.int32, (count, cycles), 1)
    spread_out = None
    for p in range(parts):
        pick = (wanted & (inner // COPIES == p)).astype(F32).astype(BF16)
        term = lax.dot_general(
            pick,
            rounded[p * lanes : (p + 1) * lanes],
            (((1,), (1,)), ((), ())),
            preferred_element_type=F32,
        )
        spread_out = term if spread_out is None else spread_out + term
    out_ref[...] = spread_out.reshape(out_ref.shape).astype(BF16)


def mix_fields(half, own, other, field_mix):
    rows, cycles = own.shape
    vmem = pl.BlockSpec(memory_space=pltpu.VMEM)
    return pl.pallas_call(
        mix_kernel,
        out_shape=jax.ShapeDtypeStruct((cycles, rows // TILE * COPIES, TILE), BF16),
        in_specs=[pl.BlockSpec(memory_space=pltpu.SMEM), vmem, vmem, vmem],
        compiler_params=pltpu.CompilerParams(vmem_limit_bytes=VMEM_LIMIT),
        name="mix_fields",
    )(half, own, other, field_mix)


def synth_kernel(
    position_ref,
    list_ref,
    coeff_ref,
    turn_ref,
    table_ref,
    out_ref,
    flip_ref,
    even_ref,
    odd_ref,
    map_ref,
    owner_ref,
    sems,
):
    position = position_ref[0]
    ring_at = position % RING
    first = position - ring_at + ring_at % SHARE
    row_copies = [
        pltpu.make_async_copy(list_ref.at[first + SHARE * k], owner_ref.at[k], sems.at[k])
        for k in range(COPIES)
    ]
    for copy in row_copies:
        copy.start()
    devices = coeff_ref.shape[0]
    groups = coeff_ref.shape[1] // COPIES
    tiles, fields = map_ref.shape[1:3]
    slots = turn_ref.shape[2]
    per_group = slots // groups
    k_half = slots * devices
    for k in range(COPIES):
        for g in range(groups):
            flip_ref[k, g] = coeff_ref[:, g * COPIES + k, :].astype(F32).T

    def one_cycle(k, lhs):
        for s in range(slots):
            at = (s % per_group) * 2 * fields
            real = flip_ref[k, s // per_group, pl.ds(at, fields), :]
            imag = flip_ref[k, s // per_group, pl.ds(at + fields, fields), :]
            for j in range(tiles):
                cos_row = turn_ref[0, j, s : s + 1, :]
                sin_row = turn_ref[1, j, s : s + 1, :]
                rows = pl.ds(j * fields, fields)
                lhs[rows, pl.ds(s * devices, devices)] = (
                    real * cos_row - imag * sin_row
                ).astype(BF16)
                lhs[rows, pl.ds(k_half + s * devices, devices)] = (
                    real * sin_row + imag * cos_row
                ).astype(BF16)
        pixels = jnp.dot(lhs[...], table_ref[...], preferred_element_type=F32).astype(BF16)
        map_ref[k] = pixels.reshape(tiles, fields, TILE)

    def cycle_pair(i, carry):
        for u, lhs in enumerate((even_ref, odd_ref)):
            one_cycle(2 * i + u, lhs)
        return carry

    lax.fori_loop(0, COPIES // 2, cycle_pair, 0)
    for copy in row_copies:
        copy.wait()
    capacity = out_ref.shape[2]
    base = ring_at - ring_at % SHARE

    def pick(t, carry):
        e = (t // SHARE) * RING + base + t % SHARE
        for k in range(COPIES):
            for c in range(capacity):
                out_ref[t, k, c] = map_ref[k, jnp.maximum(owner_ref[k, c, e], 0)]
        return carry

    lax.fori_loop(0, out_ref.shape[0], pick, 0, unroll=2)


def synthesize(position, by_slot, coeff, turns, table, fields):
    devices, capacity, _ = by_slot.shape
    tiles = turns.shape[1]
    k_total = table.shape[0]
    groups = coeff.shape[1] // COPIES
    vmem = pl.BlockSpec(memory_space=pltpu.VMEM)
    return pl.pallas_call(
        synth_kernel,
        out_shape=jax.ShapeDtypeStruct(
            (devices // COPIES, COPIES, capacity, fields, TILE), BF16
        ),
        in_specs=[
            pl.BlockSpec(memory_space=pltpu.SMEM),
            pl.BlockSpec(memory_space=pl.ANY),
            vmem,
            vmem,
            vmem,
        ],
        scratch_shapes=[
            pltpu.VMEM((COPIES, groups, TILE, devices), F32),
            pltpu.VMEM((tiles * fields, k_total), BF16),
            pltpu.VMEM((tiles * fields, k_total), BF16),
            pltpu.VMEM((COPIES, tiles, fields, TILE), BF16),
            pltpu.SMEM((COPIES, capacity, devices), jnp.int32),
            pltpu.SemaphoreType.DMA((COPIES,)),
        ],
        compiler_params=pltpu.CompilerParams(vmem_limit_bytes=VMEM_LIMIT),
        name="synthesize",
    )(position, by_slot, coeff, turns, table)


def band_kernel(row_ref, out_ref):
    rows, width = out_ref.shape[1], out_ref.shape[2]
    wide = jnp.broadcast_to(row_ref[0], (rows, width))
    out_ref[0] = pltpu.roll(wide, 0, 1, stride=1, stride_axis=0).astype(BF16)


def band_strips(rows):
    scans, _, width = rows.shape
    return pl.pallas_call(
        band_kernel,
        grid=(scans,),
        out_shape=jax.ShapeDtypeStruct((scans, HALF_BLK, width), BF16),
        in_specs=[pl.BlockSpec((1, 1, width), lambda n: (n, 0, 0))],
        out_specs=pl.BlockSpec((1, HALF_BLK, width), lambda n: (n, 0, 0)),
        compiler_params=pltpu.CompilerParams(vmem_limit_bytes=VMEM_LIMIT),
        name="band_strips",
    )(rows)


def one_hot(row):
    packed = 16
    iota = lax.broadcasted_iota(jnp.int32, (TILE, TILE), 0).astype(F32).astype(BF16)
    row = jnp.broadcast_to(row, (packed, TILE)).astype(F32).astype(BF16)
    row = jnp.concatenate([row] * (TILE // packed), axis=0)
    return jnp.where(iota == row, jnp.asarray(1, BF16), jnp.asarray(0, BF16))


def hot_kernel(pix_ref, out_ref):
    quarters = BLK // TILE

    def body(b, carry):
        for q in range(quarters):
            row = pix_ref[0, pl.ds(b * quarters + q, 1), :]
            out_ref[0, b, pl.ds(q * TILE, TILE), :] = one_hot(row).T
        return carry

    lax.fori_loop(0, out_ref.shape[1], body, 0, unroll=8)


def hot_blocks(pix):
    scans, rows, _ = pix.shape
    blocks = rows * TILE // BLK
    hots = pl.pallas_call(
        hot_kernel,
        grid=(scans,),
        out_shape=jax.ShapeDtypeStruct((scans, blocks, BLK, TILE), BF16),
        in_specs=[pl.BlockSpec((1, rows, TILE), lambda n: (n, 0, 0))],
        out_specs=pl.BlockSpec((1, blocks, BLK, TILE), lambda n: (n, 0, 0, 0)),
        compiler_params=pltpu.CompilerParams(vmem_limit_bytes=VMEM_LIMIT),
        name="hot_blocks",
    )(pix)
    return pltpu.with_memory_space_constraint(hots, pltpu.HBM)


def scan_kernel(
    list_ref,
    moved_ref,
    entry_ref,
    weight_ref,
    tiles_ref,
    pix_ref,
    strip_ref,
    hot_hbm,
    out_ref,
    pad_ref,
    wtd_ref,
    sum_ref,
    hot_ref,
    sems,
):
    scans, blocks = entry_ref.shape
    copies = [
        pltpu.make_async_copy(hot_hbm.at[n], hot_ref.at[n], sems.at[n]) for n in range(scans)
    ]
    for copy in copies:
        copy.start()
    fields = tiles_ref.shape[1]
    halves = 2 * blocks
    edge = 2 * fields
    per_half = HALF_BLK // TILE
    quarters = BLK // TILE
    sum_ref[...] = jnp.zeros_like(sum_ref)
    for p in range(2):
        pad_ref[p, pl.ds(0, edge), :] = jnp.zeros((edge, HALF_BLK), BF16)
        pad_ref[p, pl.ds(edge + halves * fields, edge), :] = jnp.zeros((edge, HALF_BLK), BF16)

    def gather(n, b):
        tile = tiles_ref[moved_ref[n, entry_ref[n, b]]].astype(F32)
        for q in range(quarters):
            at = jnp.broadcast_to(pix_ref[n, pl.ds(b * quarters + q, 1), :], (8, TILE))
            live = at >= 0
            index = jnp.maximum(at, 0)
            parts = [
                jnp.where(
                    live,
                    jnp.take_along_axis(
                        tile[8 * i : 8 * i + 8], index, axis=1, mode="promise_in_bounds"
                    ),
                    0.0,
                )
                for i in range(fields // 8)
            ]
            start = pl.multiple_of(edge + (2 * b + q // per_half) * fields, fields)
            pad_ref[
                n % 2, pl.ds(start, fields), pl.ds((q % per_half) * TILE, TILE)
            ] = jnp.concatenate(parts, axis=0).astype(BF16)

    def filter_scan(n):
        total = None
        for d in range(-2, 3):
            term = jnp.dot(
                pad_ref[n % 2, pl.ds(edge - d * fields, halves * fields), :],
                strip_ref[n, :, pl.ds((d + 2) * HALF_BLK, HALF_BLK)],
                preferred_element_type=F32,
            )
            total = term if total is None else total + term
        wtd_ref[...] = (weight_ref[n] * total).astype(BF16)

    def bin_block(n, b):
        slot = list_ref[n, entry_ref[n, b]]
        start = pl.multiple_of(2 * b * fields, fields)
        values = jnp.concatenate(
            [wtd_ref[pl.ds(start + h * fields, fields), :] for h in range(2)], axis=1
        )
        sum_ref[slot] = sum_ref[slot] + jnp.dot(
            values, hot_ref[n, b], preferred_element_type=F32
        )

    def run(body):
        lax.fori_loop(0, blocks, lambda b, carry: (body(b), carry)[1], 0, unroll=16)

    run(lambda b: gather(0, b))
    for n in range(scans):
        filter_scan(n)
        copies[n].wait()

        def both(b, n=n):
            bin_block(n, b)
            if n + 1 < scans:
                gather(n + 1, b)

        run(both)
    out_ref[...] = sum_ref[...].astype(BF16)


def scan_stage(scan_tiles, moved, block_tile, scan_weight, tiles, pix, strips, hots):
    slots, fields, _ = tiles.shape
    blocks = block_tile.shape[1]
    smem = pl.BlockSpec(memory_space=pltpu.SMEM)
    vmem = pl.BlockSpec(memory_space=pltpu.VMEM)
    return pl.pallas_call(
        scan_kernel,
        out_shape=jax.ShapeDtypeStruct((slots, fields, TILE), BF16),
        in_specs=[smem, smem, smem, smem, vmem, vmem, vmem, pl.BlockSpec(memory_space=pl.ANY)],
        out_specs=vmem,
        scratch_shapes=[
            pltpu.VMEM((2, (2 * blocks + 4) * fields, HALF_BLK), BF16),
            pltpu.VMEM((2 * blocks * fields, HALF_BLK), BF16),
            pltpu.VMEM((slots, fields, TILE), F32),
            pltpu.VMEM(hots.shape, BF16),
            pltpu.SemaphoreType.DMA((hots.shape[0],)),
        ],
        compiler_params=pltpu.CompilerParams(vmem_limit_bytes=SCAN_LIMIT),
        name="scan_stage",
    )(scan_tiles, moved, block_tile, scan_weight, tiles, pix, strips, hots)


def owner_kernel(position_ref, list_ref, back_ref, out_ref, owner_ref, sem, *sum_refs):
    row_copy = pltpu.make_async_copy(list_ref.at[position_ref[0]], owner_ref, sem)
    row_copy.start()
    capacity, devices = owner_ref.shape
    tiles = sum_refs[0].shape[0] - 1
    lanes = len(sum_refs) // capacity
    for ref in sum_refs:
        ref[...] = jnp.zeros_like(ref)
    row_copy.wait()

    def add(i, carry):
        for j in range(lanes):
            e = i * lanes + j
            for k in range(capacity):
                ref = sum_refs[j * capacity + k]
                g = owner_ref[k, e]
                g = jnp.where(g < 0, tiles, g)
                ref[g] = ref[g] + back_ref[e, k].astype(F32)
        return carry

    lax.fori_loop(0, devices // lanes, add, 0, unroll=8)
    for g in range(tiles):
        total = sum_refs[0][g]
        for ref in sum_refs[1:]:
            total = total + ref[g]
        out_ref[0, :, pl.ds(g * TILE, TILE)] = total


def owner_sum(position, by_slot, returned):
    devices, capacity, fields, _ = returned.shape
    tiles = NPHI // TILE
    return pl.pallas_call(
        owner_kernel,
        out_shape=jax.ShapeDtypeStruct((1, fields, NPHI), F32),
        in_specs=[
            pl.BlockSpec(memory_space=pltpu.SMEM),
            pl.BlockSpec(memory_space=pl.ANY),
            pl.BlockSpec(memory_space=pltpu.VMEM),
        ],
        scratch_shapes=[
            pltpu.SMEM((capacity, devices), jnp.int32),
            pltpu.SemaphoreType.DMA,
        ]
        + [pltpu.VMEM((tiles + 1, fields, TILE), F32)] * (2 * capacity),
        compiler_params=pltpu.CompilerParams(vmem_limit_bytes=VMEM_LIMIT),
        name="owner_sum",
    )(position, by_slot, returned)


def local(
    field_mix,
    alm,
    legendre,
    order_ids,
    fetch_list,
    scan_tiles,
    block_tile,
    block_pix,
    noise_kernel,
    scan_weight,
):
    half = lax.axis_index("half").reshape(1)
    position = lax.axis_index("dev").reshape(1)
    fields = alm.shape[2]
    scans = block_pix.shape[0]

    own, turns, table = contract_ells(order_ids, alm, legendre)
    other = lax.ppermute(own, "half", [(0, 1), (1, 0)])
    sent = mix_fields(half, own, other, field_mix)
    sent, block_pix, scan_tiles, noise_kernel = lax.optimization_barrier(
        (sent, block_pix, scan_tiles, noise_kernel)
    )
    coeff = lax.all_to_all(sent, "dev", split_axis=0, concat_axis=0, tiled=True)
    pix = block_pix.reshape(scans, -1, TILE)
    devices, capacity = fetch_list.shape[1:]
    source, slot = scan_tiles // capacity, scan_tiles % capacity
    member = (source // RING) * SHARE + source % SHARE
    moved = (member * COPIES + (source % RING) // SHARE) * capacity + slot

    taps = noise_kernel.astype(BF16).astype(F32)
    band = jnp.concatenate(
        [
            jnp.zeros((scans, 1), F32),
            taps[:, ::-1],
            taps[:, 1:],
            jnp.zeros((scans, HALF_BLK), F32),
        ],
        axis=1,
    )
    strips = band_strips(band[:, None, :])
    coeff, strips, pix, moved = lax.optimization_barrier((coeff, strips, pix, moved))

    by_slot = fetch_list.transpose(0, 2, 1)
    picked = synthesize(position, by_slot, coeff, turns, table, fields)
    picked, pix = lax.optimization_barrier((picked, pix))
    hots = hot_blocks(pix)
    groups = [
        [RING * q + SHARE * p + i for q in range(fetch_list.shape[0] // RING) for i in range(SHARE)]
        for p in range(COPIES)
    ]
    fetched = lax.all_to_all(
        picked, "dev", split_axis=0, concat_axis=0, tiled=True, axis_index_groups=groups
    )

    per_slot = scan_stage(
        scan_tiles,
        moved,
        block_tile,
        scan_weight,
        fetched.reshape(-1, fields, TILE),
        pix,
        strips,
        hots,
    )
    returned = lax.all_to_all(
        per_slot.reshape(devices, capacity, fields, TILE), "dev", split_axis=0, concat_axis=0, tiled=True
    )
    return owner_sum(position, by_slot, returned)


def solution(mesh):
    return jax.shard_map(
        local,
        mesh=mesh,
        in_specs=(
            P("half", None),
            P("dev", None, "half", None),
            P("dev", None, None),
            P(),
            P(),
            P("dev", None),
            P("dev", None),
            P("dev", None),
            P("dev", None),
            P("dev"),
        ),
        out_specs=P("dev", "half", None),
        check_vma=False,
    )
```
